1024 devices in a mesh: hi: 32 (over z_lo, y), lo: 32 (over x, z_hi, core).
Axes of the slice: x: 8, y: 8, z: 8 (z_hi: 2, z_lo: 4; z = z_hi * 4 + z_lo), core: 2. Of those that a mesh axis runs over, the one named last changes fastest.
Arguments:
- amplitudes: float32 [2, 1024, 512, 256], P(None, ('hi', 'lo')), may hold values from -6 to 6
- joined_gates: float32 [2, 2, 512, 512], replicated, may hold values from -0.1875 to 0.1875
- pair_gates: float32 [2, 2, 2, 2], replicated, may hold values from -3 to 3
- global_angles: float32 [2, 1024], P(None, ('hi', 'lo')), may hold values from -3.140625 to 3.140625
- local_phases: float32 [2, 17], replicated, may hold values from -3.140625 to 3.140625
- slice_bits: int32 [17], replicated, may hold values from 0 to 1
- coupled_qubits: int32 [2, 17], replicated, may hold values from 0 to 16
- gate_layout: int32 [9], replicated, may hold values from 0 to 8, each once
Outputs:
- evolved: float32 [2, 1024, 512, 256], P(None, ('hi', 'lo'))
The draws below stay inside these ranges and needn't reach their ends.
Inputs may be any that keep to these rules, and one draw needn't show every extreme that they name: `gate_layout`: each of 0 to 8 once.
All inputs are finite; a program needn't handle non-finite values.
Results may differ from the reference program's by a relative error of at most 0.0001.
Values sent between devices are 32-bit elements; how exact they have to be, the bound alone decides.
A program may use at most 32 MiB of HBM per device.

```python
import math
import jax
import jax.numpy as jnp
from jax import lax

ROW_BITS = 9
COL_BITS = 8
FIXED = 17
LAYERS = 2
ROWS = 512
COLS = 256
LQ = 17
N_HI = 32
N_LO = 32
DEVICES = 1024


def touch_ends(entries, rng, least, top_value):
    dims = entries.shape
    spot = [jax.random.randint(jax.random.fold_in(rng, axis), (), 0, dims[axis]) for axis in range(len(dims))]
    entries = entries.at[tuple(spot)].set(least)
    longest = dims.index(max(dims))
    spot[longest] = (spot[longest] + 1) % dims[longest]
    return entries.at[tuple(spot)].set(top_value)


def block_levels(own_key, dims, shards, low, top_value):
    def one(dim, parts):
        heights = jax.random.uniform(jax.random.fold_in(jax.random.fold_in(own_key, 6), dim), (parts,), jnp.float32, low / len(shards), top_value / len(shards))
        return jnp.repeat(jnp.exp(heights), dims[dim] // parts).reshape((-1,) + (1,) * (len(dims) - dim - 1))

    factor_of = one(*shards[0])
    for cut in shards[1:]:
        factor_of = factor_of * one(*cut)
    return factor_of


def bell_draw(key, dims, scale, limit, split=(), kind=jnp.bfloat16):
    factor_of = block_levels(key, dims, split, -0.22, 0.18) if split else 1.0
    entries = jax.random.normal(key, dims, jnp.float32) * scale * factor_of
    return jnp.minimum(jnp.maximum(entries, -limit), limit).astype(kind)


def setup_inputs(seed: int = 0) -> dict:
    key_of = jax.random.split(jax.random.key(seed), 9)
    return {
        "amplitudes": bell_draw(key_of[0], (2, DEVICES, ROWS, COLS), 1.0, 6.0, ((1, 1024),), jnp.float32),
        "joined_gates": bell_draw(key_of[1], (LAYERS, 2, ROWS, ROWS), (2 * ROWS) ** -0.5, 0.1875, (), jnp.float32),
        "pair_gates": bell_draw(key_of[2], (LAYERS, 2, 2, 2), 0.5, 3.0, (), jnp.float32),
        "global_angles": jnp.clip(jax.random.uniform(key_of[3], (LAYERS, DEVICES), jnp.float32, -3.140625, 3.140625), -3.140625, 3.140625),
        "local_phases": jnp.clip(jax.random.uniform(key_of[4], (LAYERS, LQ), jnp.float32, -3.140625, 3.140625), -3.140625, 3.140625),
        "slice_bits": touch_ends(jax.random.randint(key_of[5], (FIXED,), 0, 2), jax.random.fold_in(key_of[5], 1), 0, 1).astype(jnp.int32),
        "coupled_qubits": touch_ends(jax.random.randint(key_of[6], (LAYERS, FIXED), 0, LQ), jax.random.fold_in(key_of[6], 1), 0, LQ - 1).astype(jnp.int32),
        "gate_layout": jax.random.permutation(key_of[7], ROW_BITS).astype(jnp.int32),
    }


def bit_angles(angles, bit_count, length):
    positions = jnp.arange(length, dtype=jnp.int32)
    summed = jnp.zeros((length,), jnp.float32)
    for bit_pos in range(bit_count):
        chosen = ((positions >> bit_pos) & 1).astype(jnp.float32)
        summed = summed + chosen * angles[bit_pos]
    return summed


def qubit_angles(local_phases, slice_bits, coupled_qubits, layer_id):
    qubits = jnp.arange(LQ, dtype=jnp.int32)
    matches = (coupled_qubits[layer_id][:, None] == qubits[None, :]).astype(jnp.float32)
    flipped = jnp.sum(matches * slice_bits[:, None].astype(jnp.float32), axis=0)
    return local_phases[layer_id] + math.pi * flipped


def folded_gate(joined_gates, layer_id, device_angle, row_angles):
    turned = row_angles + device_angle
    cosine = jnp.cos(turned)[None, :]
    sine = jnp.sin(turned)[None, :]
    gate_real = joined_gates[layer_id, 0]
    gate_imag = joined_gates[layer_id, 1]
    return gate_real * cosine - gate_imag * sine, gate_real * sine + gate_imag * cosine


def gate_block(block, weight_real, weight_imag, col_angles):
    precise = lax.Precision.HIGHEST
    real_real = jnp.dot(weight_real, block[0], precision=precise, preferred_element_type=jnp.float32)
    real_imag = jnp.dot(weight_real, block[1], precision=precise, preferred_element_type=jnp.float32)
    imag_real = jnp.dot(weight_imag, block[0], precision=precise, preferred_element_type=jnp.float32)
    imag_imag = jnp.dot(weight_imag, block[1], precision=precise, preferred_element_type=jnp.float32)
    new_real = real_real - imag_imag
    new_imag = real_imag + imag_real
    cosine = jnp.cos(col_angles)[None, :]
    sine = jnp.sin(col_angles)[None, :]
    return jnp.stack([new_real * cosine - new_imag * sine, new_real * sine + new_imag * cosine])


def local_layer(blocks, joined_gates, global_angles, angles, layer_id):
    row_angles = bit_angles(angles[COL_BITS:], ROW_BITS, ROWS)
    col_angles = bit_angles(angles, COL_BITS, COLS)

    def one_device(pieces):
        block, device_angle = pieces
        weight_real, weight_imag = folded_gate(joined_gates, layer_id, device_angle, row_angles)
        return gate_block(block, weight_real, weight_imag, col_angles)

    return lax.map(one_device, (blocks, global_angles[layer_id]))


def pair_gate(blocks, pair_gates, layer_id, bit_pos):
    stride = 2 ** bit_pos
    shaped = blocks.reshape(DEVICES // (2 * stride), 2, stride, 2, ROWS, COLS)
    lower = shaped[:, 0]
    upper = shaped[:, 1]
    coeff_real = pair_gates[layer_id, 0]
    coeff_imag = pair_gates[layer_id, 1]
    outputs = []
    for side in range(2):
        new_real = (coeff_real[side, 0] * lower[:, :, 0] - coeff_imag[side, 0] * lower[:, :, 1]
                    + coeff_real[side, 1] * upper[:, :, 0] - coeff_imag[side, 1] * upper[:, :, 1])
        new_imag = (coeff_real[side, 0] * lower[:, :, 1] + coeff_imag[side, 0] * lower[:, :, 0]
                    + coeff_real[side, 1] * upper[:, :, 1] + coeff_imag[side, 1] * upper[:, :, 0])
        outputs.append(jnp.stack([new_real, new_imag], axis=2))
    return jnp.stack(outputs, axis=1).reshape(DEVICES, 2, ROWS, COLS)


def row_order(gate_layout):
    positions = jnp.arange(ROWS, dtype=jnp.int32)
    source = jnp.zeros((ROWS,), jnp.int32)
    for bit_pos in range(ROW_BITS):
        place = jnp.left_shift(jnp.ones((), jnp.int32), gate_layout[bit_pos].astype(jnp.int32))
        source = source + ((positions >> bit_pos) & 1) * place
    return source.astype(jnp.int32)


def remap(blocks, gate_layout):
    permuted = jnp.take(blocks, row_order(gate_layout), axis=2)
    shaped = permuted.reshape(N_HI, N_LO, 2, N_HI, ROWS // N_HI, COLS)
    return jnp.swapaxes(shaped, 0, 3).reshape(DEVICES, 2, ROWS, COLS)


def reference(amplitudes, joined_gates, pair_gates, global_angles, local_phases, slice_bits, coupled_qubits, gate_layout):
    blocks = jnp.moveaxis(amplitudes, 1, 0)
    top_bit = N_LO.bit_length() - 2
    for layer_id in range(LAYERS):
        angles = qubit_angles(local_phases, slice_bits, coupled_qubits, layer_id)
        blocks = local_layer(blocks, joined_gates, global_angles, angles, layer_id)
        blocks = pair_gate(blocks, pair_gates, layer_id, top_bit if layer_id % 2 == 0 else 0)
        if layer_id + 1 < LAYERS:
            blocks = remap(blocks, gate_layout)
    return jnp.moveaxis(blocks, 0, 1)
```

```python
import functools
import math

import jax
import jax.numpy as jnp
from jax import lax
from jax.experimental import pallas as pl
from jax.experimental.pallas import tpu as pltpu
from jax.sharding import PartitionSpec as P

MESH = pl.DeviceIdType.MESH
ROW_BITS = 9
COL_BITS = 8
FIXED = 17
LQ = 17
ROWS = 512
HALF = 128
NH = 32
NL = 32
NY = 8
NZ = 4
U = ROWS // NH
BLK = 128
NB = ROWS // BLK
TOP = NL.bit_length() - 2
X_STRIDE = 4
DY = (1, -1, 2, -2, 3, -3, 4, 0)
OFFSETS = [(dy, (at + k) % NZ) for k in range(NZ) for at, dy in enumerate(DY)]
OFFSETS = [pair for pair in OFFSETS if pair != (0, 0)]


def cmul(ar, ai, br, bi):
    return ar * br - ai * bi, ar * bi + ai * br


def turn(angle):
    return jnp.cos(angle), jnp.sin(angle)


def split(value):
    high = value.astype(jnp.bfloat16)
    return high, (value - high.astype(jnp.float32)).astype(jnp.bfloat16)


def bit_angles(angles, bit_count, positions):
    summed = jnp.zeros(positions.shape, jnp.float32)
    for bit_pos in range(bit_count):
        chosen = ((positions >> bit_pos) & 1).astype(jnp.float32)
        summed = summed + chosen * angles[bit_pos]
    return summed


def kernel(
    phases, bits, coupled, layout, pair, globals_ref, amp_hbm, gates_hbm, out_ref,
    amp, gates, turned, perm, gate0, gate1, own, msg, relay, landed, outbox, inbox, core_msg, core_in,
    high, low, load_sem, leg_send, leg_recv, all_send, all_recv, core_send, core_recv, near, mid, far,
):
    hi = lax.axis_index("hi")
    lo = lax.axis_index("lo")
    y = lax.rem(hi, NY)
    z = lax.div(hi, NY)
    top = (lo >> TOP) & 1
    bit0 = lo & 1
    x_side = (lax.rem(lo + 2 * X_STRIDE, NL), lax.rem(lo + NL - 2 * X_STRIDE, NL))
    twin = lo ^ 1

    def at(dy, dz):
        return lax.rem(z + dz, NZ) * NY + lax.rem(y + dy + NY, NY)

    loads = [
        pltpu.make_async_copy(amp_hbm, amp, load_sem.at[0]),
        pltpu.make_async_copy(gates_hbm.at[0], gates.at[0], load_sem.at[1]),
        pltpu.make_async_copy(gates_hbm.at[1], gates.at[1], load_sem.at[2]),
    ]
    for load in loads:
        load.start()

    def greet(sem, targets):
        for target in targets:
            pl.semaphore_signal(sem, inc=1, device_id=target, device_id_type=MESH)

    entry = pltpu.get_barrier_semaphore()
    neighbours = [(hi, x_side[0]), (hi, x_side[1]), (hi, twin), (at(1, 0), lo), (at(-1, 0), lo)]
    neighbours += [(at(0, dz), lo) for dz in range(1, NZ)]
    greet(entry, neighbours)

    def leg(phase, step, side, k):
        rows = pl.ds(k * BLK, BLK)
        source = (msg, relay)[step].at[phase, side, rows]
        target = (relay, landed)[step].at[phase, side, rows]
        return pltpu.make_async_remote_copy(
            src_ref=source,
            dst_ref=target,
            send_sem=leg_send.at[phase, step, side, k],
            recv_sem=leg_recv.at[phase, step, side, k],
            device_id=(hi, x_side[side]),
            device_id_type=MESH,
        )

    def core_copy(phase, k):
        rows = pl.ds(k * BLK, BLK)
        return pltpu.make_async_remote_copy(
            src_ref=core_msg.at[phase, :, rows],
            dst_ref=core_in.at[phase, :, rows],
            send_sem=core_send.at[phase, k],
            recv_sem=core_recv.at[phase, k],
            device_id=(hi, twin),
            device_id_type=MESH,
        )

    def send_all(phase):
        for dy, dz in OFFSETS:
            t = at(dy, dz)
            pltpu.make_async_remote_copy(
                src_ref=outbox.at[phase, t],
                dst_ref=inbox.at[phase, hi],
                send_sem=all_send.at[phase],
                recv_sem=all_recv.at[phase],
                device_id=(t, lo),
                device_id_type=MESH,
            ).start()
        inbox[phase, hi] = outbox[phase, hi]

    def everyone(phase):
        return pltpu.make_async_remote_copy(
            src_ref=outbox.at[phase, pl.ds(0, NH - 1)],
            dst_ref=inbox.at[phase, pl.ds(0, NH - 1)],
            send_sem=all_send.at[phase],
            recv_sem=all_recv.at[phase],
            device_id=(hi, twin),
            device_id_type=MESH,
        )

    angles = []
    for layer in range(2):
        row = []
        for q in range(LQ):
            count = jnp.int32(0)
            for f in range(FIXED):
                count = count + jnp.where(coupled[layer, f] == q, bits[f], 0)
            row.append(phases[layer, q] + math.pi * count.astype(jnp.float32))
        angles.append(row)
    row_at = lax.broadcasted_iota(jnp.int32, (1, ROWS), 1)
    row_turn = [turn(bit_angles(angles[layer][COL_BITS:], ROW_BITS, row_at)) for layer in range(2)]
    lane = lax.broadcasted_iota(jnp.int32, (1, HALF), 1)
    first_turn = turn(jnp.full((1, HALF), globals_ref[0, 0]))
    second_turn = turn(jnp.full((1, HALF), globals_ref[1, 0]))

    def coeff(layer, target_bit, source_bit):
        where = layer * 8 + target_bit * 2 + source_bit
        return pair[where], pair[where + 4]

    first_own = coeff(0, top, top)
    first_msg = coeff(0, 1 - top, top)
    last_own = []
    last_msg = []
    for phase in range(2):
        place = lane + phase * HALF
        both = cmul(
            *turn(bit_angles(angles[0], COL_BITS, place)),
            *turn(bit_angles(angles[1], COL_BITS, place)),
        )
        both = cmul(*both, *second_turn)
        last_own.append(cmul(*both, *coeff(1, bit0, bit0)))
        last_msg.append(cmul(*both, *coeff(1, 1 - bit0, bit0)))

    loads[0].wait()
    msg_factor = cmul(*first_turn, *first_msg)
    own_factor = cmul(*first_turn, *first_own)
    for k in range(NB):
        rows = pl.ds(k * BLK, BLK)
        real, imag = amp[0, 0, rows, :HALF], amp[1, 0, rows, :HALF]
        msg[0, 0, rows], msg[0, 1, rows] = cmul(real, imag, *msg_factor)
        own[0, 0, rows], own[0, 1, rows] = cmul(real, imag, *own_factor)
    pl.semaphore_wait(entry, len(neighbours))
    for k in range(NB):
        for side in range(2):
            leg(0, 0, side, k).start()
    greet(near, [(at(1, 0), lo), (at(-1, 0), lo)])

    def fill(k, real, imag):
        rows = pl.ds(k * BLK, BLK)
        high[rows, :HALF], low[rows, :HALF] = split(real)
        high[rows, HALF:], low[rows, HALF:] = split(imag)

    for k in range(NB):
        rows = pl.ds(k * BLK, BLK)
        fill(k, *cmul(amp[0, 0, rows, HALF:], amp[1, 0, rows, HALF:], *first_turn))

    def folded(layer, k):
        rows = pl.ds(pl.multiple_of(k * BLK, BLK), BLK)
        real, imag = cmul(gates[layer, 0, rows], gates[layer, 1, rows], *row_turn[layer])
        return split(real) + split(imag)

    loads[1].wait()

    def fold_first(k, carry):
        rows = pl.ds(pl.multiple_of(k * BLK, BLK), BLK)
        parts = folded(0, k)
        for kind, part in enumerate((parts[0], parts[2], parts[1], parts[3])):
            turned[rows, kind * ROWS : (kind + 1) * ROWS] = part
        return carry

    lax.fori_loop(0, NB, fold_first, 0)
    pl.semaphore_wait(near, 2)
    greet(mid, [(at(2, 0), lo), (at(-2, 0), lo)])

    def permute(k, carry):
        place = lax.broadcasted_iota(jnp.int32, (BLK, HALF), 0) + k * BLK
        source = jnp.zeros((BLK, HALF), jnp.int32)
        for bit_pos in range(ROW_BITS):
            source = source + (((place >> bit_pos) & 1) << layout[bit_pos])
        column = lax.broadcasted_iota(jnp.int32, (BLK, HALF), 1)
        for part in range(ROWS // HALF):
            hit = (source == column + part * HALF).astype(jnp.float32)
            perm[:, part * HALF : (part + 1) * HALF] = hit.astype(jnp.bfloat16)
        for kind in range(4):
            moved = jnp.dot(
                perm[...],
                turned[:, kind * ROWS : (kind + 1) * ROWS],
                preferred_element_type=jnp.float32,
            )
            gate0[k, kind * BLK : (kind + 1) * BLK] = moved.astype(jnp.bfloat16)
        return carry

    lax.fori_loop(0, NB, permute, 0)
    pl.semaphore_wait(mid, 2)
    greet(far, [(at(4, 0), lo)])

    def product(gate, k):
        main = jnp.dot(gate[k], high[...], preferred_element_type=jnp.float32)
        rest = jnp.dot(gate[k, : 2 * BLK], low[...], preferred_element_type=jnp.float32)
        real = main[:BLK] + main[2 * BLK : 3 * BLK] + rest[:BLK]
        imag = main[BLK : 2 * BLK] + main[3 * BLK :] + rest[BLK:]
        return real[:, :HALF] - imag[:, HALF:], real[:, HALF:] + imag[:, :HALF]

    def first_layer(phase):
        def block(k, carry):
            real, imag = product(gate0, k)
            spots = pl.ds(k * (BLK // U), BLK // U)
            outbox[phase, spots, 0] = real.reshape(BLK // U, U, HALF)
            outbox[phase, spots, 1] = imag.reshape(BLK // U, U, HALF)
            return carry

        lax.fori_loop(0, NB, block, 0)

    def collect(phase):
        everyone(phase).wait_recv()
        for k in range(NB):
            spots = pl.ds(k * (BLK // U), BLK // U)
            fill(
                k,
                inbox[phase, spots, 0].reshape(BLK, HALF),
                inbox[phase, spots, 1].reshape(BLK, HALF),
            )

    first_layer(1)
    pl.semaphore_wait(far, 1)
    send_all(1)

    loads[2].wait()

    def fold_second(k, carry):
        parts = folded(1, k)
        for kind, part in enumerate((parts[0], parts[2], parts[1], parts[3])):
            gate1[k, kind * BLK : (kind + 1) * BLK] = part
        return carry

    lax.fori_loop(0, NB, fold_second, 0)

    def pass_on(phase):
        for k in range(NB):
            for side in range(2):
                leg(phase, 0, side, k).wait_recv()
                leg(phase, 1, side, k).start()

    pass_on(0)

    collect(1)
    for k in range(NB):
        rows = pl.ds(k * BLK, BLK)
        real, imag = product(gate1, k)
        msg[1, 0, rows], msg[1, 1, rows] = cmul(real, imag, *first_msg)
        own[1, 0, rows], own[1, 1, rows] = cmul(real, imag, *first_own)
        for side in range(2):
            leg(1, 0, side, k).start()

    for k in range(NB):
        rows = pl.ds(k * BLK, BLK)
        for side in range(2):
            leg(0, 1, side, k).wait_recv()
        fill(k, own[0, 0, rows] + landed[0, 0, rows], own[0, 1, rows] + landed[0, 1, rows])
    first_layer(0)
    send_all(0)

    pass_on(1)

    def finish(phase, k, real, imag):
        rows = pl.ds(k * BLK, BLK)
        core_msg[phase, 0, rows], core_msg[phase, 1, rows] = cmul(real, imag, *last_msg[phase])
        core_copy(phase, k).start()
        own[phase, 0, rows], own[phase, 1, rows] = cmul(real, imag, *last_own[phase])

    def write(phase, k):
        rows = pl.ds(k * BLK, BLK)
        columns = slice(phase * HALF, (phase + 1) * HALF)
        core_copy(phase, k).wait_recv()
        for part in range(2):
            out_ref[part, rows, columns] = own[phase, part, rows] + core_in[phase, part, rows]

    collect(0)
    for k in range(NB):
        finish(0, k, *product(gate1, k))
    for k in range(NB):
        write(0, k)

    for k in range(NB):
        rows = pl.ds(k * BLK, BLK)
        for side in range(2):
            leg(1, 1, side, k).wait_recv()
        finish(1, k, own[1, 0, rows] + landed[1, 0, rows], own[1, 1, rows] + landed[1, 1, rows])
    for k in range(NB):
        write(1, k)

    for phase in range(2):
        everyone(phase).wait_send()
        for k in range(NB):
            core_copy(phase, k).wait_send()
            for step in range(2):
                for side in range(2):
                    leg(phase, step, side, k).wait_send()


def shards(
    amplitudes, joined_gates, pair_gates, global_angles, local_phases, slice_bits, coupled_qubits, gate_layout
):
    smem = pl.BlockSpec(memory_space=pltpu.SMEM)
    hbm = pl.BlockSpec(memory_space=pl.ANY)
    f32, bf16, dma = jnp.float32, jnp.bfloat16, pltpu.SemaphoreType.DMA
    half = pltpu.VMEM((2, 2, ROWS, HALF), f32)
    box = pltpu.VMEM((2, NH, 2, U, HALF), f32)
    out = pl.pallas_call(
        kernel,
        out_shape=jax.ShapeDtypeStruct((2, ROWS, 2 * HALF), f32),
        in_specs=[smem] * 6 + [hbm] * 2,
        out_specs=pl.BlockSpec(memory_space=pltpu.VMEM),
        scratch_shapes=[
            pltpu.VMEM((2, 1, ROWS, 2 * HALF), f32),
            pltpu.VMEM((2, 2, ROWS, ROWS), f32),
            pltpu.VMEM((ROWS, 4 * ROWS), bf16),
            pltpu.VMEM((BLK, ROWS), bf16),
            pltpu.VMEM((NB, 4 * BLK, ROWS), bf16),
            pltpu.VMEM((NB, 4 * BLK, ROWS), bf16),
            half, half, half, half, box, box, half, half,
            pltpu.VMEM((ROWS, 2 * HALF), bf16),
            pltpu.VMEM((ROWS, 2 * HALF), bf16),
            dma((3,)), dma((2, 2, 2, NB)), dma((2, 2, 2, NB)), dma((2,)), dma((2,)), dma((2, NB)), dma((2, NB)),
            pltpu.SemaphoreType.REGULAR, pltpu.SemaphoreType.REGULAR, pltpu.SemaphoreType.REGULAR,
        ],
        compiler_params=pltpu.CompilerParams(
            collective_id=0, has_side_effects=True, vmem_limit_bytes=56 << 20
        ),
        name="two_layers",
    )(
        local_phases, slice_bits, coupled_qubits, gate_layout, pair_gates.reshape(-1), global_angles,
        amplitudes, joined_gates,
    )
    return out[:, None]


def solution(mesh):
    placed = (
        P(None, ("hi", "lo"), None, None),
        P(),
        P(),
        P(None, ("hi", "lo")),
        P(),
        P(),
        P(),
        P(),
    )
    return jax.shard_map(
        shards,
        mesh=mesh,
        in_specs=placed,
        out_specs=P(None, ("hi", "lo"), None, None),
        check_vma=False,
    )
```

```python
import functools
import math

import jax
import jax.numpy as jnp
from jax import lax
from jax.experimental import pallas as pl
from jax.experimental.pallas import tpu as pltpu
from jax.sharding import PartitionSpec as P

MESH = pl.DeviceIdType.MESH
ROW_BITS = 9
COL_BITS = 8
FIXED = 17
LQ = 17
ROWS = 512
HALF = 128
NH = 32
NL = 32
NY = 8
NZ = 4
U = ROWS // NH
BLK = 128
NB = ROWS // BLK
TOP = NL.bit_length() - 2
X_STRIDE = 4
STEPS = 4
HOP = 4 // STEPS
DY = (1, -1, 2, -2, 3, -3, 4, 0)
OFFSETS = [(dy, (at + k) % NZ) for k in range(NZ) for at, dy in enumerate(DY)]
OFFSETS = [pair for pair in OFFSETS if pair != (0, 0)]


def cmul(ar, ai, br, bi):
    return ar * br - ai * bi, ar * bi + ai * br


def turn(angle):
    return jnp.cos(angle), jnp.sin(angle)


def split(value):
    high = value.astype(jnp.bfloat16)
    return high, (value - high.astype(jnp.float32)).astype(jnp.bfloat16)


def bit_angles(angles, bit_count, positions):
    summed = jnp.zeros(positions.shape, jnp.float32)
    for bit_pos in range(bit_count):
        chosen = ((positions >> bit_pos) & 1).astype(jnp.float32)
        summed = summed + chosen * angles[bit_pos]
    return summed


def kernel(
    phases, bits, coupled, layout, pair, globals_ref, amp_hbm, gates_hbm, out_ref,
    amp, gates, perm, gate0, gate1, own, msg, relay, landed, outbox, inbox, core_msg, core_in,
    high, low, made_high, made_low, load_sem, leg_send, leg_recv, all_send, all_recv, core_send, core_recv, near, mid, far,
):
    hi = lax.axis_index("hi")
    lo = lax.axis_index("lo")
    y = lax.rem(hi, NY)
    z = lax.div(hi, NY)
    top = (lo >> TOP) & 1
    bit0 = lo & 1
    x_side = (lax.rem(lo + HOP * X_STRIDE, NL), lax.rem(lo + NL - HOP * X_STRIDE, NL))
    twin = lo ^ 1

    def at(dy, dz):
        return lax.rem(z + dz, NZ) * NY + lax.rem(y + dy + NY, NY)

    loads = [
        pltpu.make_async_copy(amp_hbm, amp, load_sem.at[0]),
        pltpu.make_async_copy(gates_hbm.at[0], gates.at[0], load_sem.at[1]),
        pltpu.make_async_copy(gates_hbm.at[1], gates.at[1], load_sem.at[2]),
    ]
    for load in loads:
        load.start()

    def greet(sem, targets):
        for target in targets:
            pl.semaphore_signal(sem, inc=1, device_id=target, device_id_type=MESH)

    entry = pltpu.get_barrier_semaphore()
    neighbours = [(hi, x_side[0]), (hi, x_side[1]), (hi, twin), (at(1, 0), lo), (at(-1, 0), lo)]
    neighbours += [(at(0, dz), lo) for dz in range(1, NZ)]
    greet(entry, neighbours)

    def leg(phase, step, side, k):
        rows = pl.ds(k * BLK, BLK)
        places = [msg, *(relay.at[at_step] for at_step in range(STEPS - 1)), landed]
        source = places[step].at[phase, side, rows]
        target = places[step + 1].at[phase, side, rows]
        return pltpu.make_async_remote_copy(
            src_ref=source,
            dst_ref=target,
            send_sem=leg_send.at[phase, step, side, k],
            recv_sem=leg_recv.at[phase, step, side, k],
            device_id=(hi, x_side[side]),
            device_id_type=MESH,
        )

    def core_copy(phase, k):
        rows = pl.ds(k * BLK, BLK)
        return pltpu.make_async_remote_copy(
            src_ref=core_msg.at[phase, :, rows],
            dst_ref=core_in.at[phase, :, rows],
            send_sem=core_send.at[phase, k],
            recv_sem=core_recv.at[phase, k],
            device_id=(hi, twin),
            device_id_type=MESH,
        )

    def send_all(phase):
        for dy, dz in OFFSETS:
            t = at(dy, dz)
            pltpu.make_async_remote_copy(
                src_ref=outbox.at[phase, t],
                dst_ref=inbox.at[phase, hi],
                send_sem=all_send.at[phase],
                recv_sem=all_recv.at[phase],
                device_id=(t, lo),
                device_id_type=MESH,
            ).start()
        inbox[phase, hi] = outbox[phase, hi]

    def everyone(phase):
        return pltpu.make_async_remote_copy(
            src_ref=outbox.at[phase, pl.ds(0, NH - 1)],
            dst_ref=inbox.at[phase, pl.ds(0, NH - 1)],
            send_sem=all_send.at[phase],
            recv_sem=all_recv.at[phase],
            device_id=(hi, twin),
            device_id_type=MESH,
        )

    def qubit_angles(layer):
        row = []
        for q in range(LQ):
            count = jnp.int32(0)
            for f in range(FIXED):
                count = count + jnp.where(coupled[layer, f] == q, bits[f], 0)
            row.append(phases[layer, q] + math.pi * count.astype(jnp.float32))
        return row

    def row_turn(angles):
        return turn(bit_angles(angles[COL_BITS:], ROW_BITS, lax.broadcasted_iota(jnp.int32, (1, ROWS), 1)))

    def coeff(layer, target_bit, source_bit):
        return pair[layer, 0, target_bit, source_bit], pair[layer, 1, target_bit, source_bit]

    first_turn = turn(jnp.full((1, HALF), globals_ref[0, 0]))
    first_own = coeff(0, top, top)
    first_msg = coeff(0, 1 - top, top)

    def fill(k, real, imag):
        rows = pl.ds(k * BLK, BLK)
        high[rows, :HALF], low[rows, :HALF] = split(real)
        high[rows, HALF:], low[rows, HALF:] = split(imag)

    loads[0].wait()
    msg_factor = cmul(*first_turn, *first_msg)
    own_factor = cmul(*first_turn, *first_own)
    for k in range(NB):
        rows = pl.ds(k * BLK, BLK)
        real, imag = amp[0, 0, rows, :HALF], amp[1, 0, rows, :HALF]
        msg[0, 0, rows], msg[0, 1, rows] = cmul(real, imag, *msg_factor)
    pl.semaphore_wait(entry, len(neighbours))
    for k in range(NB):
        for side in range(2):
            leg(0, 0, side, k).start()
    greet(near, [(at(1, 0), lo), (at(-1, 0), lo)])

    for k in range(NB):
        rows = pl.ds(k * BLK, BLK)
        fill(k, *cmul(amp[0, 0, rows, HALF:], amp[1, 0, rows, HALF:], *first_turn))

    first_angles = qubit_angles(0)
    turned = row_turn(first_angles)

    def fold(layer, gate, factors):
        def block(k, carry):
            rows = pl.ds(pl.multiple_of(k * BLK, BLK), BLK)
            real, imag = cmul(gates[layer, 0, rows], gates[layer, 1, rows], *factors)
            parts = split(real) + split(imag)
            for kind, part in enumerate((parts[0], parts[2], parts[1], parts[3])):
                gate[k, kind * BLK : (kind + 1) * BLK] = part
            return carry

        lax.fori_loop(0, NB, block, 0)

    loads[1].wait()
    fold(0, gate0, turned)
    pl.semaphore_wait(near, 2)
    greet(mid, [(at(2, 0), lo), (at(-2, 0), lo)])

    def order(k, carry):
        place = lax.broadcasted_iota(jnp.int32, (BLK, HALF), 0) + k * BLK
        source = jnp.zeros((BLK, HALF), jnp.int32)
        for bit_pos in range(ROW_BITS):
            source = source + (((place >> bit_pos) & 1) << layout[bit_pos])
        column = lax.broadcasted_iota(jnp.int32, (BLK, HALF), 1)
        for part in range(ROWS // HALF):
            hit = (source == column + part * HALF).astype(jnp.float32)
            perm[k, :, part * HALF : (part + 1) * HALF] = hit.astype(jnp.bfloat16)
        return carry

    lax.fori_loop(0, NB, order, 0)

    def product(gate, k):
        main = jnp.dot(gate[k], high[...], preferred_element_type=jnp.float32)
        rest = jnp.dot(gate[k, : 2 * BLK], low[...], preferred_element_type=jnp.float32)
        real = main[:BLK] + main[2 * BLK : 3 * BLK] + rest[:BLK]
        imag = main[BLK : 2 * BLK] + main[3 * BLK :] + rest[BLK:]
        return real[:, :HALF] - imag[:, HALF:], real[:, HALF:] + imag[:, :HALF]

    def first_products():
        def block(k, carry):
            rows = pl.ds(pl.multiple_of(k * BLK, BLK), BLK)
            real, imag = product(gate0, k)
            made_high[rows, :HALF], made_low[rows, :HALF] = split(real)
            made_high[rows, HALF:], made_low[rows, HALF:] = split(imag)
            return carry

        lax.fori_loop(0, NB, block, 0)

    def reorder(phase):
        def block(k, carry):
            moved = jnp.dot(perm[k], made_high[...], preferred_element_type=jnp.float32)
            moved = moved + jnp.dot(perm[k], made_low[...], preferred_element_type=jnp.float32)
            spots = pl.ds(k * (BLK // U), BLK // U)
            outbox[phase, spots, 0] = moved[:, :HALF].reshape(BLK // U, U, HALF)
            outbox[phase, spots, 1] = moved[:, HALF:].reshape(BLK // U, U, HALF)
            return carry

        lax.fori_loop(0, NB, block, 0)

    def collect(phase):
        everyone(phase).wait_recv()
        for k in range(NB):
            spots = pl.ds(k * (BLK // U), BLK // U)
            fill(
                k,
                inbox[phase, spots, 0].reshape(BLK, HALF),
                inbox[phase, spots, 1].reshape(BLK, HALF),
            )

    first_products()
    pl.semaphore_wait(mid, 2)
    greet(far, [(at(4, 0), lo)])
    reorder(1)
    pl.semaphore_wait(far, 1)
    send_all(1)

    def pass_on(phase, step, k):
        for side in range(2):
            leg(phase, step - 1, side, k).wait_recv()
            leg(phase, step, side, k).start()

    for k in range(NB):
        pass_on(0, 1, k)

    for k in range(NB):
        rows = pl.ds(k * BLK, BLK)
        real, imag = amp[0, 0, rows, :HALF], amp[1, 0, rows, :HALF]
        own[0, 0, rows], own[0, 1, rows] = cmul(real, imag, *own_factor)
    second_angles = qubit_angles(1)
    loads[2].wait()
    fold(1, gate1, row_turn(second_angles))
    lane = lax.broadcasted_iota(jnp.int32, (1, HALF), 1)
    second_turn = turn(jnp.full((1, HALF), globals_ref[0, 1]))
    last_own = []
    last_msg = []
    for phase in range(2):
        place = lane + phase * HALF
        both = cmul(
            *turn(bit_angles(first_angles, COL_BITS, place)),
            *turn(bit_angles(second_angles, COL_BITS, place)),
        )
        both = cmul(*both, *second_turn)
        last_own.append(cmul(*both, *coeff(1, bit0, bit0)))
        last_msg.append(cmul(*both, *coeff(1, 1 - bit0, bit0)))

    for step in range(2, STEPS):
        for k in range(NB):
            pass_on(0, step, k)

    collect(1)
    for k in range(NB):
        rows = pl.ds(k * BLK, BLK)
        real, imag = product(gate1, k)
        msg[1, 0, rows], msg[1, 1, rows] = cmul(real, imag, *first_msg)
        own[1, 0, rows], own[1, 1, rows] = cmul(real, imag, *first_own)
        for side in range(2):
            leg(1, 0, side, k).start()

    for k in range(NB):
        rows = pl.ds(k * BLK, BLK)
        for side in range(2):
            leg(0, STEPS - 1, side, k).wait_recv()
        fill(k, own[0, 0, rows] + landed[0, 0, rows], own[0, 1, rows] + landed[0, 1, rows])
    first_products()
    reorder(0)
    send_all(0)

    for step in range(1, STEPS - 1):
        for k in range(NB):
            pass_on(1, step, k)

    def finish(phase, k, real, imag):
        rows = pl.ds(k * BLK, BLK)
        core_msg[phase, 0, rows], core_msg[phase, 1, rows] = cmul(real, imag, *last_msg[phase])
        core_copy(phase, k).start()
        own[phase, 0, rows], own[phase, 1, rows] = cmul(real, imag, *last_own[phase])

    def write(phase, k):
        rows = pl.ds(k * BLK, BLK)
        columns = slice(phase * HALF, (phase + 1) * HALF)
        core_copy(phase, k).wait_recv()
        for part in range(2):
            out_ref[part, rows, columns] = own[phase, part, rows] + core_in[phase, part, rows]

    collect(0)
    for k in range(NB):
        finish(0, k, *product(gate1, k))
        pass_on(1, STEPS - 1, k)
    for k in range(NB):
        write(0, k)

    for k in range(NB):
        rows = pl.ds(k * BLK, BLK)
        for side in range(2):
            leg(1, STEPS - 1, side, k).wait_recv()
        finish(1, k, own[1, 0, rows] + landed[1, 0, rows], own[1, 1, rows] + landed[1, 1, rows])
    for k in range(NB):
        write(1, k)

    for phase in range(2):
        everyone(phase).wait_send()
        for k in range(NB):
            core_copy(phase, k).wait_send()
            for step in range(STEPS):
                for side in range(2):
                    leg(phase, step, side, k).wait_send()


def shards(
    amplitudes, joined_gates, pair_gates, global_angles, local_phases, slice_bits, coupled_qubits, gate_layout
):
    smem = pl.BlockSpec(memory_space=pltpu.SMEM)
    hbm = pl.BlockSpec(memory_space=pltpu.HBM)
    f32, bf16, dma = jnp.float32, jnp.bfloat16, pltpu.SemaphoreType.DMA
    half = pltpu.VMEM((2, 2, ROWS, HALF), f32)
    box = pltpu.VMEM((2, NH, 2, U, HALF), f32)
    out = pl.pallas_call(
        kernel,
        out_shape=jax.ShapeDtypeStruct((2, ROWS, 2 * HALF), f32),
        in_specs=[smem] * 6 + [hbm] * 2,
        out_specs=pl.BlockSpec(memory_space=pltpu.VMEM),
        scratch_shapes=[
            pltpu.VMEM((2, 1, ROWS, 2 * HALF), f32),
            pltpu.VMEM((2, 2, ROWS, ROWS), f32),
            pltpu.VMEM((NB, BLK, ROWS), bf16),
            pltpu.VMEM((NB, 4 * BLK, ROWS), bf16),
            pltpu.VMEM((NB, 4 * BLK, ROWS), bf16),
            half, half, pltpu.VMEM((STEPS - 1, 2, 2, ROWS, HALF), f32), half, box, box, half, half,
            *[pltpu.VMEM((ROWS, 2 * HALF), bf16)] * 4,
            dma((3,)), dma((2, STEPS, 2, NB)), dma((2, STEPS, 2, NB)), dma((2,)), dma((2,)), dma((2, NB)), dma((2, NB)),
            pltpu.SemaphoreType.REGULAR, pltpu.SemaphoreType.REGULAR, pltpu.SemaphoreType.REGULAR,
        ],
        compiler_params=pltpu.CompilerParams(
            collective_id=0, has_side_effects=True, vmem_limit_bytes=58 << 20
        ),
        name="two_layers",
    )(
        local_phases, slice_bits, coupled_qubits, gate_layout, pair_gates, global_angles.T,
        amplitudes, joined_gates,
    )
    return out[:, None]


def solution(mesh):
    placed = (
        P(None, ("hi", "lo"), None, None),
        P(),
        P(),
        P(None, ("hi", "lo")),
        P(),
        P(),
        P(),
        P(),
    )
    return jax.shard_map(
        shards,
        mesh=mesh,
        in_specs=placed,
        out_specs=P(None, ("hi", "lo"), None, None),
        check_vma=False,
    )
```

```python
import functools
import math

import jax
import jax.numpy as jnp
from jax import lax
from jax.experimental import pallas as pl
from jax.experimental.pallas import tpu as pltpu
from jax.sharding import PartitionSpec as P

MESH = pl.DeviceIdType.MESH
ROW_BITS = 9
COL_BITS = 8
FIXED = 17
LQ = 17
ROWS = 512
HALF = 128
NH = 32
NL = 32
NY = 8
NZ = 4
U = ROWS // NH
BLK = 128
NB = ROWS // BLK
TOP = NL.bit_length() - 2
X_STRIDE = 4
STEPS = 4
HOP = 4 // STEPS
DY = (1, -1, 2, -2, 3, -3, 4, 0)
OFFSETS = [(dy, (at + k) % NZ) for k in range(NZ) for at, dy in enumerate(DY)]
OFFSETS = [pair for pair in OFFSETS if pair != (0, 0)]


def cmul(ar, ai, br, bi):
    return ar * br - ai * bi, ar * bi + ai * br


def turn(angle):
    return jnp.cos(angle), jnp.sin(angle)


def split(value):
    high = value.astype(jnp.bfloat16)
    return high, (value - high.astype(jnp.float32)).astype(jnp.bfloat16)


def bit_angles(angles, bit_count, positions):
    summed = jnp.zeros(positions.shape, jnp.float32)
    for bit_pos in range(bit_count):
        chosen = ((positions >> bit_pos) & 1).astype(jnp.float32)
        summed = summed + chosen * angles[bit_pos]
    return summed


def kernel(
    phases, bits, coupled, layout, pair, globals_ref, amp_hbm, gates_hbm, out_ref,
    amp, gates, perm, gate0, gate1, own, msg, relay, landed, outbox, inbox, core_msg, core_in,
    high, low, made_high, made_low, load_sem, leg_send, leg_recv, all_send, all_recv, core_send, core_recv, near, mid, far,
):
    hi = lax.axis_index("hi")
    lo = lax.axis_index("lo")
    y = lax.rem(hi, NY)
    z = lax.div(hi, NY)
    top = (lo >> TOP) & 1
    bit0 = lo & 1
    x_side = (lax.rem(lo + HOP * X_STRIDE, NL), lax.rem(lo + NL - HOP * X_STRIDE, NL))
    twin = lo ^ 1

    def at(dy, dz):
        return lax.rem(z + dz, NZ) * NY + lax.rem(y + dy + NY, NY)

    loads = [
        pltpu.make_async_copy(amp_hbm, amp, load_sem.at[0]),
        pltpu.make_async_copy(gates_hbm.at[0], gates.at[0], load_sem.at[1]),
        pltpu.make_async_copy(gates_hbm.at[1], gates.at[1], load_sem.at[2]),
    ]
    for load in loads[:2]:
        load.start()

    def greet(sem, targets):
        for target in targets:
            pl.semaphore_signal(sem, inc=1, device_id=target, device_id_type=MESH)

    entry = pltpu.get_barrier_semaphore()
    neighbours = [(hi, x_side[0]), (hi, x_side[1]), (hi, twin), (at(1, 0), lo), (at(-1, 0), lo)]
    neighbours += [(at(0, dz), lo) for dz in range(1, NZ)]
    greet(entry, neighbours)

    def leg(phase, step, side, k):
        rows = pl.ds(k * BLK, BLK)
        places = [msg, *(relay.at[at_step] for at_step in range(STEPS - 1)), landed]
        source = places[step].at[phase, side, rows]
        target = places[step + 1].at[phase, side, rows]
        return pltpu.make_async_remote_copy(
            src_ref=source,
            dst_ref=target,
            send_sem=leg_send.at[phase, step, side, k],
            recv_sem=leg_recv.at[phase, step, side, k],
            device_id=(hi, x_side[side]),
            device_id_type=MESH,
        )

    def core_copy(phase, k):
        rows = pl.ds(k * BLK, BLK)
        return pltpu.make_async_remote_copy(
            src_ref=core_msg.at[phase, :, rows],
            dst_ref=core_in.at[phase, :, rows],
            send_sem=core_send.at[phase, k],
            recv_sem=core_recv.at[phase, k],
            device_id=(hi, twin),
            device_id_type=MESH,
        )

    def send_all(phase):
        for dy, dz in OFFSETS:
            t = at(dy, dz)
            pltpu.make_async_remote_copy(
                src_ref=outbox.at[phase, t],
                dst_ref=inbox.at[phase, hi],
                send_sem=all_send.at[phase],
                recv_sem=all_recv.at[phase],
                device_id=(t, lo),
                device_id_type=MESH,
            ).start()
        inbox[phase, hi] = outbox[phase, hi]

    def everyone(phase):
        return pltpu.make_async_remote_copy(
            src_ref=outbox.at[phase, pl.ds(0, NH - 1)],
            dst_ref=inbox.at[phase, pl.ds(0, NH - 1)],
            send_sem=all_send.at[phase],
            recv_sem=all_recv.at[phase],
            device_id=(hi, twin),
            device_id_type=MESH,
        )

    def qubit_angles(layer):
        row = []
        for q in range(LQ):
            count = jnp.int32(0)
            for f in range(FIXED):
                count = count + jnp.where(coupled[layer, f] == q, bits[f], 0)
            row.append(phases[layer, q] + math.pi * count.astype(jnp.float32))
        return row

    def row_turn(angles):
        return turn(bit_angles(angles[COL_BITS:], ROW_BITS, lax.broadcasted_iota(jnp.int32, (1, ROWS), 1)))

    def coeff(layer, target_bit, source_bit):
        return pair[layer, 0, target_bit, source_bit], pair[layer, 1, target_bit, source_bit]

    first_turn = turn(jnp.full((1, HALF), globals_ref[0, 0]))
    first_own = coeff(0, top, top)
    first_msg = coeff(0, 1 - top, top)

    def fill(k, real, imag):
        rows = pl.ds(k * BLK, BLK)
        high[rows, :HALF], low[rows, :HALF] = split(real)
        high[rows, HALF:], low[rows, HALF:] = split(imag)

    def order(k, carry):
        place = lax.broadcasted_iota(jnp.int32, (BLK, HALF), 0) + k * BLK
        source = jnp.zeros((BLK, HALF), jnp.int32)
        for bit_pos in range(ROW_BITS):
            source = source + (((place >> bit_pos) & 1) << layout[bit_pos])
        column = lax.broadcasted_iota(jnp.int32, (BLK, HALF), 1)
        for part in range(ROWS // HALF):
            hit = (source == column + part * HALF).astype(jnp.float32)
            perm[k, :, part * HALF : (part + 1) * HALF] = hit.astype(jnp.bfloat16)
        return carry

    lax.fori_loop(0, NB, order, 0)

    first_angles = qubit_angles(0)
    turned = row_turn(first_angles)

    loads[0].wait()
    msg_factor = cmul(*first_turn, *first_msg)
    own_factor = cmul(*first_turn, *first_own)
    for k in range(NB):
        rows = pl.ds(k * BLK, BLK)
        real, imag = amp[0, 0, rows, :HALF], amp[1, 0, rows, :HALF]
        msg[0, 0, rows], msg[0, 1, rows] = cmul(real, imag, *msg_factor)
    pl.semaphore_wait(entry, len(neighbours))
    for k in range(NB):
        for side in range(2):
            leg(0, 0, side, k).start()
    greet(near, [(at(1, 0), lo), (at(-1, 0), lo)])

    for k in range(NB):
        rows = pl.ds(k * BLK, BLK)
        fill(k, *cmul(amp[0, 0, rows, HALF:], amp[1, 0, rows, HALF:], *first_turn))

    def fold(layer, gate, factors):
        def block(k, carry):
            rows = pl.ds(pl.multiple_of(k * BLK, BLK), BLK)
            real, imag = cmul(gates[layer, 0, rows], gates[layer, 1, rows], *factors)
            parts = split(real) + split(imag)
            for kind, part in enumerate((parts[0], parts[2], parts[1], parts[3])):
                gate[k, kind * BLK : (kind + 1) * BLK] = part
            return carry

        lax.fori_loop(0, NB, block, 0)

    loads[1].wait()
    loads[2].start()
    fold(0, gate0, turned)
    pl.semaphore_wait(near, 2)
    greet(mid, [(at(2, 0), lo), (at(-2, 0), lo)])

    def product(gate, k):
        main = jnp.dot(gate[k], high[...], preferred_element_type=jnp.float32)
        rest = jnp.dot(gate[k, : 2 * BLK], low[...], preferred_element_type=jnp.float32)
        real = main[:BLK] + main[2 * BLK : 3 * BLK] + rest[:BLK]
        imag = main[BLK : 2 * BLK] + main[3 * BLK :] + rest[BLK:]
        return real[:, :HALF] - imag[:, HALF:], real[:, HALF:] + imag[:, :HALF]

    def first_products():
        def block(k, carry):
            rows = pl.ds(pl.multiple_of(k * BLK, BLK), BLK)
            real, imag = product(gate0, k)
            made_high[rows, :HALF], made_low[rows, :HALF] = split(real)
            made_high[rows, HALF:], made_low[rows, HALF:] = split(imag)
            return carry

        lax.fori_loop(0, NB, block, 0)

    def reorder(phase):
        def block(k, carry):
            moved = jnp.dot(perm[k], made_high[...], preferred_element_type=jnp.float32)
            moved = moved + jnp.dot(perm[k], made_low[...], preferred_element_type=jnp.float32)
            spots = pl.ds(k * (BLK // U), BLK // U)
            outbox[phase, spots, 0] = moved[:, :HALF].reshape(BLK // U, U, HALF)
            outbox[phase, spots, 1] = moved[:, HALF:].reshape(BLK // U, U, HALF)
            return carry

        lax.fori_loop(0, NB, block, 0)

    def collect(phase):
        everyone(phase).wait_recv()
        for k in range(NB):
            spots = pl.ds(k * (BLK // U), BLK // U)
            fill(
                k,
                inbox[phase, spots, 0].reshape(BLK, HALF),
                inbox[phase, spots, 1].reshape(BLK, HALF),
            )

    first_products()
    pl.semaphore_wait(mid, 2)
    greet(far, [(at(4, 0), lo)])
    reorder(1)
    pl.semaphore_wait(far, 1)
    send_all(1)

    def pass_on(phase, step, k):
        for side in range(2):
            leg(phase, step - 1, side, k).wait_recv()
            leg(phase, step, side, k).start()

    for k in range(NB):
        pass_on(0, 1, k)

    for k in range(NB):
        rows = pl.ds(k * BLK, BLK)
        real, imag = amp[0, 0, rows, :HALF], amp[1, 0, rows, :HALF]
        own[0, 0, rows], own[0, 1, rows] = cmul(real, imag, *own_factor)
    second_angles = qubit_angles(1)
    loads[2].wait()
    fold(1, gate1, row_turn(second_angles))
    lane = lax.broadcasted_iota(jnp.int32, (1, HALF), 1)
    second_turn = turn(jnp.full((1, HALF), globals_ref[0, 1]))
    last_own = []
    last_msg = []
    for phase in range(2):
        place = lane + phase * HALF
        both = cmul(
            *turn(bit_angles(first_angles, COL_BITS, place)),
            *turn(bit_angles(second_angles, COL_BITS, place)),
        )
        both = cmul(*both, *second_turn)
        last_own.append(cmul(*both, *coeff(1, bit0, bit0)))
        last_msg.append(cmul(*both, *coeff(1, 1 - bit0, bit0)))

    for step in range(2, STEPS):
        for k in range(NB):
            pass_on(0, step, k)

    collect(1)
    for k in range(NB):
        rows = pl.ds(k * BLK, BLK)
        real, imag = product(gate1, k)
        msg[1, 0, rows], msg[1, 1, rows] = cmul(real, imag, *first_msg)
        own[1, 0, rows], own[1, 1, rows] = cmul(real, imag, *first_own)
        for side in range(2):
            leg(1, 0, side, k).start()

    for k in range(NB):
        rows = pl.ds(k * BLK, BLK)
        for side in range(2):
            leg(0, STEPS - 1, side, k).wait_recv()
        fill(k, own[0, 0, rows] + landed[0, 0, rows], own[0, 1, rows] + landed[0, 1, rows])
    first_products()
    reorder(0)
    send_all(0)

    for step in range(1, STEPS):
        for k in range(NB):
            pass_on(1, step, k)

    def finish(phase, k, real, imag):
        rows = pl.ds(k * BLK, BLK)
        core_msg[phase, 0, rows], core_msg[phase, 1, rows] = cmul(real, imag, *last_msg[phase])
        core_copy(phase, k).start()
        own[phase, 0, rows], own[phase, 1, rows] = cmul(real, imag, *last_own[phase])

    def write(phase, k):
        rows = pl.ds(k * BLK, BLK)
        columns = slice(phase * HALF, (phase + 1) * HALF)
        core_copy(phase, k).wait_recv()
        for part in range(2):
            out_ref[part, rows, columns] = own[phase, part, rows] + core_in[phase, part, rows]

    collect(0)
    for k in range(NB):
        finish(0, k, *product(gate1, k))
    for k in range(NB):
        write(0, k)

    for k in range(NB):
        rows = pl.ds(k * BLK, BLK)
        for side in range(2):
            leg(1, STEPS - 1, side, k).wait_recv()
        finish(1, k, own[1, 0, rows] + landed[1, 0, rows], own[1, 1, rows] + landed[1, 1, rows])
    for k in range(NB):
        write(1, k)

    for phase in range(2):
        everyone(phase).wait_send()
        for k in range(NB):
            core_copy(phase, k).wait_send()
            for step in range(STEPS):
                for side in range(2):
                    leg(phase, step, side, k).wait_send()


def shards(
    amplitudes, joined_gates, pair_gates, global_angles, local_phases, slice_bits, coupled_qubits, gate_layout
):
    smem = pl.BlockSpec(memory_space=pltpu.SMEM)
    hbm = pl.BlockSpec(memory_space=pltpu.HBM)
    f32, bf16, dma = jnp.float32, jnp.bfloat16, pltpu.SemaphoreType.DMA
    half = pltpu.VMEM((2, 2, ROWS, HALF), f32)
    box = pltpu.VMEM((2, NH, 2, U, HALF), f32)
    out = pl.pallas_call(
        kernel,
        out_shape=jax.ShapeDtypeStruct((2, ROWS, 2 * HALF), f32),
        in_specs=[smem] * 6 + [hbm] * 2,
        out_specs=pl.BlockSpec(memory_space=pltpu.VMEM),
        scratch_shapes=[
            pltpu.VMEM((2, 1, ROWS, 2 * HALF), f32),
            pltpu.VMEM((2, 2, ROWS, ROWS), f32),
            pltpu.VMEM((NB, BLK, ROWS), bf16),
            pltpu.VMEM((NB, 4 * BLK, ROWS), bf16),
            pltpu.VMEM((NB, 4 * BLK, ROWS), bf16),
            half, half, pltpu.VMEM((STEPS - 1, 2, 2, ROWS, HALF), f32), half, box, box, half, half,
            *[pltpu.VMEM((ROWS, 2 * HALF), bf16)] * 4,
            dma((3,)), dma((2, STEPS, 2, NB)), dma((2, STEPS, 2, NB)), dma((2,)), dma((2,)), dma((2, NB)), dma((2, NB)),
            pltpu.SemaphoreType.REGULAR, pltpu.SemaphoreType.REGULAR, pltpu.SemaphoreType.REGULAR,
        ],
        compiler_params=pltpu.CompilerParams(
            collective_id=0, has_side_effects=True, vmem_limit_bytes=40 << 20
        ),
        name="two_layers",
    )(
        *(
            pltpu.with_memory_space_constraint(array, pltpu.HBM)
            for array in (
                local_phases, slice_bits, coupled_qubits, gate_layout, pair_gates, global_angles.T,
                amplitudes, joined_gates,
            )
        ),
    )
    return out[:, None]


def solution(mesh):
    placed = (
        P(None, ("hi", "lo"), None, None),
        P(),
        P(),
        P(None, ("hi", "lo")),
        P(),
        P(),
        P(),
        P(),
    )
    return jax.shard_map(
        shards,
        mesh=mesh,
        in_specs=placed,
        out_specs=P(None, ("hi", "lo"), None, None),
        check_vma=False,
    )
```

```python
import functools
import math

import jax
import jax.numpy as jnp
from jax import lax
from jax.experimental import pallas as pl
from jax.experimental.pallas import tpu as pltpu
from jax.sharding import PartitionSpec as P

MESH = pl.DeviceIdType.MESH
ROW_BITS = 9
COL_BITS = 8
FIXED = 17
LQ = 17
ROWS = 512
HALF = 128
NH = 32
NL = 32
NY = 8
NZ = 4
U = ROWS // NH
BLK = 128
NB = ROWS // BLK
TOP = NL.bit_length() - 2
X_STRIDE = 4
STEPS = 4
HOP = 4 // STEPS
RELAYS = sorted(
    ((step, k) for step in range(1, STEPS) for k in range(NB)), key=lambda item: (item[1] + 2 * item[0], item[0])
)
DY = (1, -1, 2, -2, 3, -3, 4, 0)
OFFSETS = [(dy, (at + k) % NZ) for k in range(NZ) for at, dy in enumerate(DY)]
OFFSETS = [pair for pair in OFFSETS if pair != (0, 0)]


def cmul(ar, ai, br, bi):
    return ar * br - ai * bi, ar * bi + ai * br


def turn(angle):
    return jnp.cos(angle), jnp.sin(angle)


def split(value):
    high = value.astype(jnp.bfloat16)
    return high, (value - high.astype(jnp.float32)).astype(jnp.bfloat16)


def bit_angles(angles, bit_count, positions):
    summed = jnp.zeros(positions.shape, jnp.float32)
    for bit_pos in range(bit_count):
        chosen = ((positions >> bit_pos) & 1).astype(jnp.float32)
        summed = summed + chosen * angles[bit_pos]
    return summed


def kernel(
    phases, bits, coupled, layout, pair, globals_ref, amp_hbm, gates_hbm, out_ref,
    amp, gates, perm, gate0, gate1, own, msg, relay, landed, outbox, inbox, core_msg, core_in,
    high, low, made_high, made_low, load_sem, leg_send, leg_recv, all_send, all_recv, core_send, core_recv, near, mid, far,
):
    hi = lax.axis_index("hi")
    lo = lax.axis_index("lo")
    y = lax.rem(hi, NY)
    z = lax.div(hi, NY)
    top = (lo >> TOP) & 1
    bit0 = lo & 1
    x_side = (lax.rem(lo + HOP * X_STRIDE, NL), lax.rem(lo + NL - HOP * X_STRIDE, NL))
    twin = lo ^ 1

    def at(dy, dz):
        return lax.rem(z + dz, NZ) * NY + lax.rem(y + dy + NY, NY)

    loads = [
        pltpu.make_async_copy(amp_hbm, amp, load_sem.at[0]),
        pltpu.make_async_copy(gates_hbm.at[0], gates.at[0], load_sem.at[1]),
        pltpu.make_async_copy(gates_hbm.at[1], gates.at[1], load_sem.at[2]),
    ]
    for load in loads[:2]:
        load.start()

    def greet(sem, targets):
        for target in targets:
            pl.semaphore_signal(sem, inc=1, device_id=target, device_id_type=MESH)

    entry = pltpu.get_barrier_semaphore()
    neighbours = [(hi, x_side[0]), (hi, x_side[1]), (hi, twin), (at(1, 0), lo), (at(-1, 0), lo)]
    neighbours += [(at(0, dz), lo) for dz in range(1, NZ)]
    greet(entry, neighbours)

    def leg(phase, step, side, k):
        rows = pl.ds(k * BLK, BLK)
        places = [msg, *(relay.at[at_step] for at_step in range(STEPS - 1)), landed]
        source = places[step].at[phase, side, rows]
        target = places[step + 1].at[phase, side, rows]
        return pltpu.make_async_remote_copy(
            src_ref=source,
            dst_ref=target,
            send_sem=leg_send.at[phase, step, side, k],
            recv_sem=leg_recv.at[phase, step, side, k],
            device_id=(hi, x_side[side]),
            device_id_type=MESH,
        )

    def core_copy(phase, k):
        rows = pl.ds(k * BLK, BLK)
        return pltpu.make_async_remote_copy(
            src_ref=core_msg.at[phase, :, rows],
            dst_ref=core_in.at[phase, :, rows],
            send_sem=core_send.at[phase, k],
            recv_sem=core_recv.at[phase, k],
            device_id=(hi, twin),
            device_id_type=MESH,
        )

    def send_all(phase):
        for dy, dz in OFFSETS:
            t = at(dy, dz)
            pltpu.make_async_remote_copy(
                src_ref=outbox.at[phase, t],
                dst_ref=inbox.at[phase, hi],
                send_sem=all_send.at[phase],
                recv_sem=all_recv.at[phase],
                device_id=(t, lo),
                device_id_type=MESH,
            ).start()
        inbox[phase, hi] = outbox[phase, hi]

    def everyone(phase):
        return pltpu.make_async_remote_copy(
            src_ref=outbox.at[phase, pl.ds(0, NH - 1)],
            dst_ref=inbox.at[phase, pl.ds(0, NH - 1)],
            send_sem=all_send.at[phase],
            recv_sem=all_recv.at[phase],
            device_id=(hi, twin),
            device_id_type=MESH,
        )

    def qubit_angles(layer):
        row = []
        for q in range(LQ):
            count = jnp.int32(0)
            for f in range(FIXED):
                count = count + jnp.where(coupled[layer, f] == q, bits[f], 0)
            row.append(phases[layer, q] + math.pi * count.astype(jnp.float32))
        return row

    def row_turn(angles):
        return turn(bit_angles(angles[COL_BITS:], ROW_BITS, lax.broadcasted_iota(jnp.int32, (1, ROWS), 1)))

    def coeff(layer, target_bit, source_bit):
        return pair[layer, 0, target_bit, source_bit], pair[layer, 1, target_bit, source_bit]

    first_turn = turn(jnp.full((1, HALF), globals_ref[0, 0]))
    first_own = coeff(0, top, top)
    first_msg = coeff(0, 1 - top, top)

    def fill(k, real, imag):
        rows = pl.ds(k * BLK, BLK)
        high[rows, :HALF], low[rows, :HALF] = split(real)
        high[rows, HALF:], low[rows, HALF:] = split(imag)

    def order(k, carry):
        place = lax.broadcasted_iota(jnp.int32, (BLK, HALF), 0) + k * BLK
        source = jnp.zeros((BLK, HALF), jnp.int32)
        for bit_pos in range(ROW_BITS):
            source = source + (((place >> bit_pos) & 1) << layout[bit_pos])
        column = lax.broadcasted_iota(jnp.int32, (BLK, HALF), 1)
        for part in range(ROWS // HALF):
            hit = (source == column + part * HALF).astype(jnp.float32)
            perm[k, :, part * HALF : (part + 1) * HALF] = hit.astype(jnp.bfloat16)
        return carry

    lax.fori_loop(0, NB, order, 0)

    first_angles = qubit_angles(0)
    turned = row_turn(first_angles)

    loads[0].wait()
    msg_factor = cmul(*first_turn, *first_msg)
    own_factor = cmul(*first_turn, *first_own)
    for k in range(NB):
        rows = pl.ds(k * BLK, BLK)
        real, imag = amp[0, 0, rows, :HALF], amp[1, 0, rows, :HALF]
        msg[0, 0, rows], msg[0, 1, rows] = cmul(real, imag, *msg_factor)
    pl.semaphore_wait(entry, len(neighbours))
    for k in range(NB):
        for side in range(2):
            leg(0, 0, side, k).start()
    greet(near, [(at(1, 0), lo), (at(-1, 0), lo)])

    for k in range(NB):
        rows = pl.ds(k * BLK, BLK)
        fill(k, *cmul(amp[0, 0, rows, HALF:], amp[1, 0, rows, HALF:], *first_turn))

    def fold(layer, gate, factors):
        def block(k, carry):
            rows = pl.ds(pl.multiple_of(k * BLK, BLK), BLK)
            real, imag = cmul(gates[layer, 0, rows], gates[layer, 1, rows], *factors)
            parts = split(real) + split(imag)
            for kind, part in enumerate((parts[0], parts[2], parts[1], parts[3])):
                gate[k, kind * BLK : (kind + 1) * BLK] = part
            return carry

        lax.fori_loop(0, NB, block, 0)

    loads[1].wait()
    loads[2].start()
    fold(0, gate0, turned)
    pl.semaphore_wait(near, 2)
    greet(mid, [(at(2, 0), lo), (at(-2, 0), lo)])

    def product(gate, k):
        main = jnp.dot(gate[k], high[...], preferred_element_type=jnp.float32)
        rest = jnp.dot(gate[k, : 2 * BLK], low[...], preferred_element_type=jnp.float32)
        real = main[:BLK] + main[2 * BLK : 3 * BLK] + rest[:BLK]
        imag = main[BLK : 2 * BLK] + main[3 * BLK :] + rest[BLK:]
        return real[:, :HALF] - imag[:, HALF:], real[:, HALF:] + imag[:, :HALF]

    def first_products():
        def block(k, carry):
            rows = pl.ds(pl.multiple_of(k * BLK, BLK), BLK)
            real, imag = product(gate0, k)
            made_high[rows, :HALF], made_low[rows, :HALF] = split(real)
            made_high[rows, HALF:], made_low[rows, HALF:] = split(imag)
            return carry

        lax.fori_loop(0, NB, block, 0)

    def reorder(phase):
        def block(k, carry):
            moved = jnp.dot(perm[k], made_high[...], preferred_element_type=jnp.float32)
            moved = moved + jnp.dot(perm[k], made_low[...], preferred_element_type=jnp.float32)
            spots = pl.ds(k * (BLK // U), BLK // U)
            outbox[phase, spots, 0] = moved[:, :HALF].reshape(BLK // U, U, HALF)
            outbox[phase, spots, 1] = moved[:, HALF:].reshape(BLK // U, U, HALF)
            return carry

        lax.fori_loop(0, NB, block, 0)

    def collect(phase):
        everyone(phase).wait_recv()
        for k in range(NB):
            spots = pl.ds(k * (BLK // U), BLK // U)
            fill(
                k,
                inbox[phase, spots, 0].reshape(BLK, HALF),
                inbox[phase, spots, 1].reshape(BLK, HALF),
            )

    first_products()
    pl.semaphore_wait(mid, 2)
    greet(far, [(at(4, 0), lo)])
    reorder(1)
    pl.semaphore_wait(far, 1)
    send_all(1)

    def pass_on(phase, step, k):
        for side in range(2):
            leg(phase, step - 1, side, k).wait_recv()
            leg(phase, step, side, k).start()

    for step, k in RELAYS[:3]:
        pass_on(0, step, k)

    for k in range(NB):
        rows = pl.ds(k * BLK, BLK)
        real, imag = amp[0, 0, rows, :HALF], amp[1, 0, rows, :HALF]
        own[0, 0, rows], own[0, 1, rows] = cmul(real, imag, *own_factor)
    second_angles = qubit_angles(1)
    loads[2].wait()
    fold(1, gate1, row_turn(second_angles))
    lane = lax.broadcasted_iota(jnp.int32, (1, HALF), 1)
    second_turn = turn(jnp.full((1, HALF), globals_ref[0, 1]))
    last_own = []
    last_msg = []
    for phase in range(2):
        place = lane + phase * HALF
        both = cmul(
            *turn(bit_angles(first_angles, COL_BITS, place)),
            *turn(bit_angles(second_angles, COL_BITS, place)),
        )
        both = cmul(*both, *second_turn)
        last_own.append(cmul(*both, *coeff(1, bit0, bit0)))
        last_msg.append(cmul(*both, *coeff(1, 1 - bit0, bit0)))

    for step, k in RELAYS[3:]:
        pass_on(0, step, k)

    collect(1)
    for k in range(NB):
        rows = pl.ds(k * BLK, BLK)
        real, imag = product(gate1, k)
        msg[1, 0, rows], msg[1, 1, rows] = cmul(real, imag, *first_msg)
        own[1, 0, rows], own[1, 1, rows] = cmul(real, imag, *first_own)
        for side in range(2):
            leg(1, 0, side, k).start()

    for k in range(NB):
        rows = pl.ds(k * BLK, BLK)
        for side in range(2):
            leg(0, STEPS - 1, side, k).wait_recv()
        fill(k, own[0, 0, rows] + landed[0, 0, rows], own[0, 1, rows] + landed[0, 1, rows])
    first_products()
    reorder(0)
    send_all(0)

    for step, k in RELAYS:
        pass_on(1, step, k)

    def finish(phase, k, real, imag):
        rows = pl.ds(k * BLK, BLK)
        core_msg[phase, 0, rows], core_msg[phase, 1, rows] = cmul(real, imag, *last_msg[phase])
        core_copy(phase, k).start()
        own[phase, 0, rows], own[phase, 1, rows] = cmul(real, imag, *last_own[phase])

    def write(phase, k):
        rows = pl.ds(k * BLK, BLK)
        columns = slice(phase * HALF, (phase + 1) * HALF)
        core_copy(phase, k).wait_recv()
        for part in range(2):
            out_ref[part, rows, columns] = own[phase, part, rows] + core_in[phase, part, rows]

    collect(0)
    for k in range(NB):
        finish(0, k, *product(gate1, k))
    for k in range(NB):
        write(0, k)

    for k in range(NB):
        rows = pl.ds(k * BLK, BLK)
        for side in range(2):
            leg(1, STEPS - 1, side, k).wait_recv()
        finish(1, k, own[1, 0, rows] + landed[1, 0, rows], own[1, 1, rows] + landed[1, 1, rows])
    for k in range(NB):
        write(1, k)

    for phase in range(2):
        everyone(phase).wait_send()
        for k in range(NB):
            core_copy(phase, k).wait_send()
            for step in range(STEPS):
                for side in range(2):
                    leg(phase, step, side, k).wait_send()


def shards(
    amplitudes, joined_gates, pair_gates, global_angles, local_phases, slice_bits, coupled_qubits, gate_layout
):
    smem = pl.BlockSpec(memory_space=pltpu.SMEM)
    hbm = pl.BlockSpec(memory_space=pltpu.HBM)
    f32, bf16, dma = jnp.float32, jnp.bfloat16, pltpu.SemaphoreType.DMA
    half = pltpu.VMEM((2, 2, ROWS, HALF), f32)
    box = pltpu.VMEM((2, NH, 2, U, HALF), f32)
    out = pl.pallas_call(
        kernel,
        out_shape=jax.ShapeDtypeStruct((2, ROWS, 2 * HALF), f32),
        in_specs=[smem] * 6 + [hbm] * 2,
        out_specs=pl.BlockSpec(memory_space=pltpu.VMEM),
        scratch_shapes=[
            pltpu.VMEM((2, 1, ROWS, 2 * HALF), f32),
            pltpu.VMEM((2, 2, ROWS, ROWS), f32),
            pltpu.VMEM((NB, BLK, ROWS), bf16),
            pltpu.VMEM((NB, 4 * BLK, ROWS), bf16),
            pltpu.VMEM((NB, 4 * BLK, ROWS), bf16),
            half, half, pltpu.VMEM((STEPS - 1, 2, 2, ROWS, HALF), f32), half, box, box, half, half,
            *[pltpu.VMEM((ROWS, 2 * HALF), bf16)] * 4,
            dma((3,)), dma((2, STEPS, 2, NB)), dma((2, STEPS, 2, NB)), dma((2,)), dma((2,)), dma((2, NB)), dma((2, NB)),
            pltpu.SemaphoreType.REGULAR, pltpu.SemaphoreType.REGULAR, pltpu.SemaphoreType.REGULAR,
        ],
        compiler_params=pltpu.CompilerParams(
            collective_id=0, has_side_effects=True, vmem_limit_bytes=40 << 20
        ),
        name="two_layers",
    )(
        *(
            pltpu.with_memory_space_constraint(array, pltpu.HBM)
            for array in (
                local_phases, slice_bits, coupled_qubits, gate_layout, pair_gates, global_angles.T,
                amplitudes, joined_gates,
            )
        ),
    )
    return out[:, None]


def solution(mesh):
    placed = (
        P(None, ("hi", "lo"), None, None),
        P(),
        P(),
        P(None, ("hi", "lo")),
        P(),
        P(),
        P(),
        P(),
    )
    return jax.shard_map(
        shards,
        mesh=mesh,
        in_specs=placed,
        out_specs=P(None, ("hi", "lo"), None, None),
        check_vma=False,
    )
```

```python
import functools
import math

import jax
import jax.numpy as jnp
from jax import lax
from jax.experimental import pallas as pl
from jax.experimental.pallas import tpu as pltpu
from jax.sharding import PartitionSpec as P

MESH = pl.DeviceIdType.MESH
ROW_BITS = 9
COL_BITS = 8
FIXED = 17
LQ = 17
ROWS = 512
HALF = 128
NH = 32
NL = 32
NY = 8
NZ = 4
U = ROWS // NH
BLK = 128
NB = ROWS // BLK
TOP = NL.bit_length() - 2
X_STRIDE = 4
STEPS = 4
HOP = 4 // STEPS
DY = (1, -1, 2, -2, 3, -3, 4, 0)
OFFSETS = [(dy, (at + k) % NZ) for k in range(NZ) for at, dy in enumerate(DY)]
OFFSETS = [pair for pair in OFFSETS if pair != (0, 0)]


def cmul(ar, ai, br, bi):
    return ar * br - ai * bi, ar * bi + ai * br


def turn(angle):
    return jnp.cos(angle), jnp.sin(angle)


def split(value):
    high = value.astype(jnp.bfloat16)
    return high, (value - high.astype(jnp.float32)).astype(jnp.bfloat16)


def bit_angles(angles, bit_count, positions):
    summed = jnp.zeros(positions.shape, jnp.float32)
    for bit_pos in range(bit_count):
        chosen = ((positions >> bit_pos) & 1).astype(jnp.float32)
        summed = summed + chosen * angles[bit_pos]
    return summed


def kernel(
    phases, bits, coupled, layout, pair, globals_ref, amp_hbm, gates_hbm, out_ref,
    amp, gates, perm, gate0, gate1, own, msg, relay, landed, outbox, inbox, core_msg, core_in,
    high, low, made_high, made_low, load_sem, leg_send, leg_recv, all_send, all_recv, core_send, core_recv, near, mid, far,
):
    hi = lax.axis_index("hi")
    lo = lax.axis_index("lo")
    y = lax.rem(hi, NY)
    z = lax.div(hi, NY)
    top = (lo >> TOP) & 1
    bit0 = lo & 1
    x_side = (lax.rem(lo + HOP * X_STRIDE, NL), lax.rem(lo + NL - HOP * X_STRIDE, NL))
    twin = lo ^ 1

    def at(dy, dz):
        return lax.rem(z + dz, NZ) * NY + lax.rem(y + dy + NY, NY)

    loads = [
        pltpu.make_async_copy(amp_hbm, amp, load_sem.at[0]),
        pltpu.make_async_copy(gates_hbm.at[0], gates.at[0], load_sem.at[1]),
        pltpu.make_async_copy(gates_hbm.at[1], gates.at[1], load_sem.at[2]),
    ]
    for load in loads[:2]:
        load.start()

    def greet(sem, targets):
        for target in targets:
            pl.semaphore_signal(sem, inc=1, device_id=target, device_id_type=MESH)

    entry = pltpu.get_barrier_semaphore()
    neighbours = [(hi, x_side[0]), (hi, x_side[1]), (hi, twin), (at(1, 0), lo), (at(-1, 0), lo)]
    neighbours += [(at(0, dz), lo) for dz in range(1, NZ)]
    greet(entry, neighbours)

    def leg(phase, step, side, k):
        rows = pl.ds(k * BLK, BLK)
        places = [msg, *(relay.at[at_step] for at_step in range(STEPS - 1)), landed]
        source = places[step].at[phase, side, rows]
        target = places[step + 1].at[phase, side, rows]
        return pltpu.make_async_remote_copy(
            src_ref=source,
            dst_ref=target,
            send_sem=leg_send.at[phase, step, side, k],
            recv_sem=leg_recv.at[phase, step, side, k],
            device_id=(hi, x_side[side]),
            device_id_type=MESH,
        )

    def core_copy(phase, k):
        rows = pl.ds(k * BLK, BLK)
        return pltpu.make_async_remote_copy(
            src_ref=core_msg.at[phase, :, rows],
            dst_ref=core_in.at[phase, :, rows],
            send_sem=core_send.at[phase, k],
            recv_sem=core_recv.at[phase, k],
            device_id=(hi, twin),
            device_id_type=MESH,
        )

    def send_all(phase):
        for dy, dz in OFFSETS:
            t = at(dy, dz)
            pltpu.make_async_remote_copy(
                src_ref=outbox.at[phase, t],
                dst_ref=inbox.at[phase, hi],
                send_sem=all_send.at[phase],
                recv_sem=all_recv.at[phase],
                device_id=(t, lo),
                device_id_type=MESH,
            ).start()
        inbox[phase, hi] = outbox[phase, hi]

    def everyone(phase):
        return pltpu.make_async_remote_copy(
            src_ref=outbox.at[phase, pl.ds(0, NH - 1)],
            dst_ref=inbox.at[phase, pl.ds(0, NH - 1)],
            send_sem=all_send.at[phase],
            recv_sem=all_recv.at[phase],
            device_id=(hi, twin),
            device_id_type=MESH,
        )

    def qubit_angles(layer):
        row = []
        for q in range(LQ):
            count = jnp.int32(0)
            for f in range(FIXED):
                count = count + jnp.where(coupled[layer, f] == q, bits[f], 0)
            row.append(phases[layer, q] + math.pi * count.astype(jnp.float32))
        return row

    def row_turn(angles):
        return turn(bit_angles(angles[COL_BITS:], ROW_BITS, lax.broadcasted_iota(jnp.int32, (1, ROWS), 1)))

    def coeff(layer, target_bit, source_bit):
        return pair[layer, 0, target_bit, source_bit], pair[layer, 1, target_bit, source_bit]

    first_turn = turn(jnp.full((1, HALF), globals_ref[0, 0]))
    first_own = coeff(0, top, top)
    first_msg = coeff(0, 1 - top, top)

    def fill(k, real, imag):
        rows = pl.ds(k * BLK, BLK)
        high[rows, :HALF], low[rows, :HALF] = split(real)
        high[rows, HALF:], low[rows, HALF:] = split(imag)

    loads[0].wait()
    msg_factor = cmul(*first_turn, *first_msg)
    own_factor = cmul(*first_turn, *first_own)
    for k in range(NB):
        rows = pl.ds(k * BLK, BLK)
        real, imag = amp[0, 0, rows, :HALF], amp[1, 0, rows, :HALF]
        msg[0, 0, rows], msg[0, 1, rows] = cmul(real, imag, *msg_factor)
    pl.semaphore_wait(entry, len(neighbours))
    for k in range(NB):
        for side in range(2):
            leg(0, 0, side, k).start()
    greet(near, [(at(1, 0), lo), (at(-1, 0), lo)])

    def order(k, carry):
        place = lax.broadcasted_iota(jnp.int32, (BLK, HALF), 0) + k * BLK
        source = jnp.zeros((BLK, HALF), jnp.int32)
        for bit_pos in range(ROW_BITS):
            source = source + (((place >> bit_pos) & 1) << layout[bit_pos])
        column = lax.broadcasted_iota(jnp.int32, (BLK, HALF), 1)
        for part in range(ROWS // HALF):
            hit = (source == column + part * HALF).astype(jnp.float32)
            perm[k, :, part * HALF : (part + 1) * HALF] = hit.astype(jnp.bfloat16)
        return carry

    lax.fori_loop(0, NB, order, 0)

    first_angles = qubit_angles(0)
    turned = row_turn(first_angles)

    for k in range(NB):
        rows = pl.ds(k * BLK, BLK)
        fill(k, *cmul(amp[0, 0, rows, HALF:], amp[1, 0, rows, HALF:], *first_turn))

    def fold(layer, gate, factors):
        def block(k, carry):
            rows = pl.ds(pl.multiple_of(k * BLK, BLK), BLK)
            real, imag = cmul(gates[layer, 0, rows], gates[layer, 1, rows], *factors)
            parts = split(real) + split(imag)
            for kind, part in enumerate((parts[0], parts[2], parts[1], parts[3])):
                gate[k, kind * BLK : (kind + 1) * BLK] = part
            return carry

        lax.fori_loop(0, NB, block, 0)

    loads[1].wait()
    loads[2].start()
    fold(0, gate0, turned)
    pl.semaphore_wait(near, 2)
    greet(mid, [(at(2, 0), lo), (at(-2, 0), lo)])

    def product(gate, k):
        main = jnp.dot(gate[k], high[...], preferred_element_type=jnp.float32)
        rest = jnp.dot(gate[k, : 2 * BLK], low[...], preferred_element_type=jnp.float32)
        real = main[:BLK] + main[2 * BLK : 3 * BLK] + rest[:BLK]
        imag = main[BLK : 2 * BLK] + main[3 * BLK :] + rest[BLK:]
        return real[:, :HALF] - imag[:, HALF:], real[:, HALF:] + imag[:, :HALF]

    def first_products():
        def block(k, carry):
            rows = pl.ds(pl.multiple_of(k * BLK, BLK), BLK)
            real, imag = product(gate0, k)
            made_high[rows, :HALF], made_low[rows, :HALF] = split(real)
            made_high[rows, HALF:], made_low[rows, HALF:] = split(imag)
            return carry

        lax.fori_loop(0, NB, block, 0)

    def reorder(phase):
        def block(k, carry):
            moved = jnp.dot(perm[k], made_high[...], preferred_element_type=jnp.float32)
            moved = moved + jnp.dot(perm[k], made_low[...], preferred_element_type=jnp.float32)
            spots = pl.ds(k * (BLK // U), BLK // U)
            outbox[phase, spots, 0] = moved[:, :HALF].reshape(BLK // U, U, HALF)
            outbox[phase, spots, 1] = moved[:, HALF:].reshape(BLK // U, U, HALF)
            return carry

        lax.fori_loop(0, NB, block, 0)

    def collect(phase):
        everyone(phase).wait_recv()
        for k in range(NB):
            spots = pl.ds(k * (BLK // U), BLK // U)
            fill(
                k,
                inbox[phase, spots, 0].reshape(BLK, HALF),
                inbox[phase, spots, 1].reshape(BLK, HALF),
            )

    first_products()
    pl.semaphore_wait(mid, 2)
    greet(far, [(at(4, 0), lo)])
    reorder(1)
    pl.semaphore_wait(far, 1)
    send_all(1)

    def pass_on(phase, step, k):
        for side in range(2):
            leg(phase, step - 1, side, k).wait_recv()
            leg(phase, step, side, k).start()

    for k in range(NB):
        pass_on(0, 1, k)

    for k in range(NB):
        rows = pl.ds(k * BLK, BLK)
        real, imag = amp[0, 0, rows, :HALF], amp[1, 0, rows, :HALF]
        own[0, 0, rows], own[0, 1, rows] = cmul(real, imag, *own_factor)
    second_angles = qubit_angles(1)
    loads[2].wait()
    fold(1, gate1, row_turn(second_angles))
    lane = lax.broadcasted_iota(jnp.int32, (1, HALF), 1)
    second_turn = turn(jnp.full((1, HALF), globals_ref[0, 1]))
    last_own = []
    last_msg = []
    for phase in range(2):
        place = lane + phase * HALF
        both = cmul(
            *turn(bit_angles(first_angles, COL_BITS, place)),
            *turn(bit_angles(second_angles, COL_BITS, place)),
        )
        both = cmul(*both, *second_turn)
        last_own.append(cmul(*both, *coeff(1, bit0, bit0)))
        last_msg.append(cmul(*both, *coeff(1, 1 - bit0, bit0)))

    for step in range(2, STEPS):
        for k in range(NB):
            pass_on(0, step, k)

    collect(1)
    for k in range(NB):
        rows = pl.ds(k * BLK, BLK)
        real, imag = product(gate1, k)
        msg[1, 0, rows], msg[1, 1, rows] = cmul(real, imag, *first_msg)
        own[1, 0, rows], own[1, 1, rows] = cmul(real, imag, *first_own)
        for side in range(2):
            leg(1, 0, side, k).start()

    for k in range(NB):
        rows = pl.ds(k * BLK, BLK)
        for side in range(2):
            leg(0, STEPS - 1, side, k).wait_recv()
        fill(k, own[0, 0, rows] + landed[0, 0, rows], own[0, 1, rows] + landed[0, 1, rows])
    first_products()
    reorder(0)
    send_all(0)

    for step in range(1, STEPS):
        for k in range(NB):
            pass_on(1, step, k)

    def finish(phase, k, real, imag):
        rows = pl.ds(k * BLK, BLK)
        core_msg[phase, 0, rows], core_msg[phase, 1, rows] = cmul(real, imag, *last_msg[phase])
        core_copy(phase, k).start()
        own[phase, 0, rows], own[phase, 1, rows] = cmul(real, imag, *last_own[phase])

    def write(phase, k):
        rows = pl.ds(k * BLK, BLK)
        columns = slice(phase * HALF, (phase + 1) * HALF)
        core_copy(phase, k).wait_recv()
        for part in range(2):
            out_ref[part, rows, columns] = own[phase, part, rows] + core_in[phase, part, rows]

    collect(0)
    for k in range(NB):
        finish(0, k, *product(gate1, k))
    for k in range(NB):
        write(0, k)

    for k in range(NB):
        rows = pl.ds(k * BLK, BLK)
        for side in range(2):
            leg(1, STEPS - 1, side, k).wait_recv()
        finish(1, k, own[1, 0, rows] + landed[1, 0, rows], own[1, 1, rows] + landed[1, 1, rows])
    for k in range(NB):
        write(1, k)

    for phase in range(2):
        everyone(phase).wait_send()
        for k in range(NB):
            core_copy(phase, k).wait_send()
            for step in range(STEPS):
                for side in range(2):
                    leg(phase, step, side, k).wait_send()


def shards(
    amplitudes, joined_gates, pair_gates, global_angles, local_phases, slice_bits, coupled_qubits, gate_layout
):
    smem = pl.BlockSpec(memory_space=pltpu.SMEM)
    hbm = pl.BlockSpec(memory_space=pltpu.HBM)
    f32, bf16, dma = jnp.float32, jnp.bfloat16, pltpu.SemaphoreType.DMA
    half = pltpu.VMEM((2, 2, ROWS, HALF), f32)
    box = pltpu.VMEM((2, NH, 2, U, HALF), f32)
    out = pl.pallas_call(
        kernel,
        out_shape=jax.ShapeDtypeStruct((2, ROWS, 2 * HALF), f32),
        in_specs=[smem] * 6 + [hbm] * 2,
        out_specs=pl.BlockSpec(memory_space=pltpu.VMEM),
        scratch_shapes=[
            pltpu.VMEM((2, 1, ROWS, 2 * HALF), f32),
            pltpu.VMEM((2, 2, ROWS, ROWS), f32),
            pltpu.VMEM((NB, BLK, ROWS), bf16),
            pltpu.VMEM((NB, 4 * BLK, ROWS), bf16),
            pltpu.VMEM((NB, 4 * BLK, ROWS), bf16),
            half, half, pltpu.VMEM((STEPS - 1, 2, 2, ROWS, HALF), f32), half, box, box, half, half,
            *[pltpu.VMEM((ROWS, 2 * HALF), bf16)] * 4,
            dma((3,)), dma((2, STEPS, 2, NB)), dma((2, STEPS, 2, NB)), dma((2,)), dma((2,)), dma((2, NB)), dma((2, NB)),
            pltpu.SemaphoreType.REGULAR, pltpu.SemaphoreType.REGULAR, pltpu.SemaphoreType.REGULAR,
        ],
        compiler_params=pltpu.CompilerParams(
            collective_id=0, has_side_effects=True, vmem_limit_bytes=40 << 20
        ),
        name="two_layers",
    )(
        *(
            pltpu.with_memory_space_constraint(array, pltpu.HBM)
            for array in (
                local_phases, slice_bits, coupled_qubits, gate_layout, pair_gates, global_angles.T,
                amplitudes, joined_gates,
            )
        ),
    )
    return out[:, None]


def solution(mesh):
    placed = (
        P(None, ("hi", "lo"), None, None),
        P(),
        P(),
        P(None, ("hi", "lo")),
        P(),
        P(),
        P(),
        P(),
    )
    return jax.shard_map(
        shards,
        mesh=mesh,
        in_specs=placed,
        out_specs=P(None, ("hi", "lo"), None, None),
        check_vma=False,
    )
```
